128 devices in a mesh: dp: 8 (over x_lo, z), cell: 16 (over x_hi, y, core).
Axes of the slice: x: 4 (x_hi: 2, x_lo: 2; x = x_hi * 2 + x_lo), y: 4, z: 4, core: 2. Of those that a mesh axis runs over, the one named last changes fastest.
Arguments:
- sensitivity: float32 [4096, 65536], P(('dp', 'cell')), may hold values from -0.09375 to 0.09375
- row_period: int32 [4096], P(('dp', 'cell')), may hold values from 0 to 31
- row_site: int32 [4096], P(('dp', 'cell')), may hold values from 0 to 127
- period_err: float32 [32], replicated, may hold values from 0.2 to 2
- site_err: float32 [128], replicated, may hold values from 0.2 to 2
- cell_var: float32 [65536], replicated, may hold values from 0.25 to 4
- cell_perm: int32 [65536], replicated, may hold values from 0 to 65535, each once
Outputs:
- gram: float32 [4096, 4096], P('cell', 'dp')
The draws below stay inside these ranges and needn't reach their ends.
Inputs may be any that keep to these rules, and one draw needn't show every extreme that they name: `cell_perm`: a permutation of 0 to 65535.
All inputs are finite; a program needn't handle non-finite values.
Results may differ from the reference program's by a relative error of at most 0.0009.
Values may be sent and summed in bfloat16 or wider, within the bound.
No kernel may reach another device: no remote copies, remote signals or barrier semaphores. Data moves between devices by JAX's collectives and lax.ppermute only.
A program may use at most 128 MiB of HBM per device.

```python
import math
import jax
import jax.numpy as jnp
from jax import lax

NCELL = 65536
NPER = 32
NSITE = 128
ND = 4096


def set_ends(drawn, rng, low, top_value):
    longest = drawn.shape.index(max(drawn.shape))
    spots = []
    for shift in (0, 1):
        where = [jax.random.randint(jax.random.fold_in(rng, axis), (), 0, length) for axis, length in enumerate(drawn.shape)]
        where[longest] = (where[longest] + shift) % drawn.shape[longest]
        spots.append(tuple(where))
    return drawn.at[spots[0]].set(low).at[spots[1]].set(top_value)


def with_spikes(entries, stream_key, source, target, blocks, factor):
    def block_of(dim):
        return (jnp.arange(entries.shape[dim]) // (entries.shape[dim] // blocks)).reshape((-1,) + (1,) * (entries.ndim - 1 - dim))

    first = jax.random.permutation(stream_key, blocks)[block_of(target)]
    second = (block_of(target) + blocks // 2) % blocks
    return jnp.where((block_of(source) == first) | (block_of(source) == second), factor * entries, entries)


def block_scale(rng, shape, split, low, top_value):
    gain, own = 1.0, jax.random.fold_in(rng, 6)
    for dim, blocks in split:
        heights = jnp.exp(jax.random.uniform(jax.random.fold_in(own, dim), (blocks,), jnp.float32, low / len(split), top_value / len(split)))
        gain = gain * jnp.repeat(heights, shape[dim] // blocks).reshape([-1 if axis == dim else 1 for axis in range(len(shape))])
    return gain


def heavy_noise(key, dims, spread, reach, cuts, heavy, kind=jnp.bfloat16):
    array = spread * jax.random.normal(key, dims, jnp.float32)
    if cuts:
        array = array * block_scale(key, dims, cuts, -0.22, 0.18)
    return jnp.clip(with_spikes(array, jax.random.fold_in(key, 3), *heavy), -reach, reach).astype(kind)


def setup_inputs(seed: int = 0) -> dict:
    streams_of = jax.random.split(jax.random.key(seed), 8)
    return {
        "sensitivity": heavy_noise(streams_of[0], (ND, NCELL), NCELL ** -0.5, 0.09375, ((0, 128),), (1, 0, 128, 5.5), jnp.float32),
        "row_period": set_ends(jax.random.randint(streams_of[1], (ND,), 0, NPER), jax.random.fold_in(streams_of[1], 1), 0, NPER - 1).astype(jnp.int32),
        "row_site": set_ends(jax.random.randint(streams_of[2], (ND,), 0, NSITE), jax.random.fold_in(streams_of[2], 1), 0, NSITE - 1).astype(jnp.int32),
        "period_err": jnp.clip(jnp.exp(jax.random.uniform(streams_of[3], (NPER,), jnp.float32, math.log(0.2), math.log(2.0))), 0.2, 2.0),
        "site_err": jnp.clip(jnp.exp(jax.random.uniform(streams_of[4], (NSITE,), jnp.float32, math.log(0.2), math.log(2.0))), 0.2, 2.0),
        "cell_var": jnp.clip(jnp.exp(jax.random.uniform(streams_of[5], (NCELL,), jnp.float32, math.log(0.25), math.log(4.0))), 0.25, 4.0),
        "cell_perm": jax.random.permutation(streams_of[6], NCELL).astype(jnp.int32),
    }


def reference(sensitivity, row_period, row_site, period_err, site_err, cell_var, cell_perm):
    period_scale = period_err[row_period]
    site_scale = site_err[row_site]
    row_weight = 1.0 / jnp.sqrt(period_scale * period_scale + site_scale * site_scale)
    scaled = (row_weight[:, None] * sensitivity).astype(jnp.bfloat16)
    column_var = cell_var[cell_perm]
    weighted = (scaled.astype(jnp.float32) * column_var[None, :]).astype(jnp.bfloat16)
    return lax.dot_general(scaled, weighted, (((1,), (1,)), ((), ())), preferred_element_type=jnp.float32)
```

```python
import functools

import jax
import jax.numpy as jnp
from jax import lax
from jax.experimental import pallas as pl
from jax.experimental.pallas import tpu as pltpu
from jax.sharding import Mesh, PartitionSpec as P

AXES = ("xl", "z", "xh", "y", "core")
SIZES = (2, 4, 2, 4, 2)
PLANE = ("z", "y", "core")
RING = ("xl", "xh", "core")
CHUNKS = 2
INTERPRET = False


def row_weights(row_period, row_site, period_err, site_err):
    period_hit = row_period[:, None] == jnp.arange(period_err.shape[0], dtype=jnp.int32)[None, :]
    site_hit = row_site[:, None] == jnp.arange(site_err.shape[0], dtype=jnp.int32)[None, :]
    period_scale = jnp.sum(jnp.where(period_hit, period_err[None, :], 0.0), axis=1)
    site_scale = jnp.sum(jnp.where(site_hit, site_err[None, :], 0.0), axis=1)
    return 1.0 / jnp.sqrt(period_scale * period_scale + site_scale * site_scale)


def flat(xl, z, xh, y, core):
    return (((xl * 4 + z) * 2 + xh) * 4 + y) * 2 + core


def ring_index(x, core):
    return ((x % 2) * 2 + x // 2) * 2 + core


def to_ring_neighbour():
    pairs = []
    for x in range(4):
        pairs.append((ring_index((x + 1) % 4, 0), ring_index(x, 0)))
        pairs.append((ring_index((x - 1) % 4, 1), ring_index(x, 1)))
    return pairs


def plane_shift(shift, first):
    pairs = []
    for z in range(4):
        for y in range(4):
            for core in range(2):
                along_y = (core == 0) == first
                to_z, to_y = (z, (y + shift) % 4) if along_y else ((z + shift) % 4, y)
                pairs.append(((z * 4 + y) * 2 + core, (to_z * 4 + to_y) * 2 + core))
    return pairs


def homes(place):
    pairs = []
    for xl in range(2):
        for z in range(4):
            for xh in range(2):
                for y in range(4):
                    for core in range(2):
                        source = place(xl, z, xh, y, core)
                        if source is not None:
                            pairs.append((flat(*source), flat(xl, z, xh, y, core)))
    return pairs


def near_source(half, mirrored):
    def place(xl, z, xh, y, core):
        if xh == xl:
            return None
        forward = (2 * core + xh - (2 * half + xl)) % 4 == 1
        holder = 0 if forward else 1
        if mirrored:
            return (xh, y, core, z, 1 - holder)
        return (xl, z, half, y, holder)

    return place


def own_source(part):
    return lambda xl, z, xh, y, core: (xl, z, core, y, part) if xh == xl else None


def far_source(part, mirrored):
    def place(xl, z, xh, y, core):
        if xh != xl:
            return None
        return (xl, y, core, z, part) if mirrored else (xl, z, 1 - core, y, part)

    return place


def tile_kernel(scal_ref, *refs, chunks):
    lhs, rhs, outs = refs[:chunks], refs[chunks : 2 * chunks], refs[2 * chunks :]
    total = None
    for a, b in zip(lhs, rhs):
        part = lax.dot_general(
            a[...], b[...], (((1,), (1,)), ((), ())), preferred_element_type=jnp.float32
        )
        total = part if total is None else total + part
    step = pl.program_id(0)
    if len(outs) == 1:
        outs[0][...] = total.reshape(outs[0].shape)
    else:
        for index, out in enumerate(outs):

            @pl.when(step == index)
            def _(out=out):
                out[...] = total.reshape(out.shape)


def tile_products(lhs, rhs, scalars, split, joined, windowed):
    rows, depth = lhs[0].shape
    tile = rows // 4
    height = tile // 2 if split else tile

    def lhs_map(s, v, scal):
        r = lax.rem(scal[0] + jnp.where(scal[2] == 0, s, v), 4)
        return (2 * r + scal[3], 0) if split else (r, 0)

    def rhs_map(s, v, scal):
        c = lax.rem(scal[1] + jnp.where(scal[2] == 0, v, s), 4)
        return (c, scal[4]) if windowed else (c, 0)

    if joined:
        out_shape = [jax.ShapeDtypeStruct((4, 4, height, tile), jnp.float32)]
        out_specs = [pl.BlockSpec((1, 1, height, tile), lambda s, v, scal: (s, v, 0, 0))]
    else:
        out_shape = [jax.ShapeDtypeStruct((4, height, tile), jnp.float32)] * 4
        out_specs = [
            pl.BlockSpec(
                (1, height, tile),
                lambda s, v, scal, i=i: (jnp.where(s < i, 0, jnp.where(s == i, v, 3)), 0, 0),
            )
            for i in range(4)
        ]
    chunks = len(lhs)
    return pl.pallas_call(
        functools.partial(tile_kernel, chunks=chunks),
        out_shape=out_shape,
        grid_spec=pltpu.PrefetchScalarGridSpec(
            num_scalar_prefetch=1,
            grid=(4, 4),
            in_specs=[pl.BlockSpec((height, depth), lhs_map)] * chunks
            + [pl.BlockSpec((tile, depth), rhs_map)] * chunks,
            out_specs=out_specs,
        ),
        compiler_params=pltpu.CompilerParams(dimension_semantics=("arbitrary", "arbitrary")),
        cost_estimate=pl.CostEstimate(
            flops=2 * 16 * height * tile * depth * chunks,
            bytes_accessed=16 * height * tile * 4 + chunks * (height * 4 + rows) * depth * 2,
            transcendentals=0,
        ),
        interpret=INTERPRET,
    )(scalars, *lhs, *rhs)


def reduce_plane(strips):
    total = strips[0]
    for shift in (1, 3, 2):
        total = total + lax.ppermute(strips[shift], PLANE, plane_shift(shift, True))
    tile = total[0]
    for shift in (1, 3, 2):
        tile = tile + lax.ppermute(total[shift], PLANE, plane_shift(shift, False))
    return tile


def swap_cores(value):
    return lax.ppermute(value, "core", [(0, 1), (1, 0)])


def body(sensitivity, row_period, row_site, period_err, site_err, cell_var, cell_perm):
    xl, z, xh, y, core = (lax.axis_index(name).astype(jnp.int32) for name in AXES)
    x = 2 * xh + xl
    cells = cell_var.shape[0]
    chunk = cells // CHUNKS
    depth = chunk // 32
    weight = row_weights(row_period, row_site, period_err, site_err)[:, None]

    scaled = []
    for j in range(CHUNKS):
        packed = (weight * sensitivity[:, j * chunk : (j + 1) * chunk]).astype(jnp.bfloat16)
        scaled.append(lax.all_to_all(packed, PLANE, split_axis=1, concat_axis=0, tiled=True))

    first = ((z * 4 + y) * 2 + core) * depth
    positions = jnp.concatenate(
        [lax.dynamic_slice_in_dim(cell_perm, j * chunk + first, depth) for j in range(CHUNKS)]
    )
    column_var = cell_var[positions]
    weighted = [
        (scaled[j].astype(jnp.float32) * column_var[None, j * depth : (j + 1) * depth]).astype(
            jnp.bfloat16
        )
        for j in range(CHUNKS)
    ]

    near = [lax.ppermute(part, RING, to_ring_neighbour()) for part in scaled]
    window = x // 2
    target = lax.rem(x + jnp.where(core == 0, 3, 1), 4)
    far = [
        lax.ppermute(
            lax.dynamic_slice_in_dim(part, (target // 2) * (depth // 2), depth // 2, 1),
            RING,
            to_ring_neighbour(),
        )
        for part in near
    ]

    def scalars(order, half):
        return jnp.stack([y, z, order, half, window]).astype(jnp.int32)

    def halves(lhs, windowed):
        sent = tile_products(lhs, weighted, scalars(1 - core, 1 - core), True, True, windowed)[0]
        kept = tile_products(lhs, weighted, scalars(core, core), True, False, windowed)
        got = swap_cores(sent)
        return reduce_plane([kept[s] + got[s] for s in range(4)])

    own_tile = halves(scaled, False)
    near_tile = reduce_plane(tile_products(near, weighted, scalars(core, 0 * core), False, False, False))
    far_tile = halves(far, True)

    def fetch(value, place):
        return lax.ppermute(value, AXES, homes(place))

    own = jnp.concatenate([fetch(own_tile, own_source(part)) for part in (0, 1)], axis=0)
    near_tiles = [
        fetch(near_tile, near_source(half, False)) + fetch(near_tile, near_source(half, True)).T
        for half in (0, 1)
    ]
    far_whole = (
        jnp.concatenate([fetch(far_tile, far_source(part, False)) for part in (0, 1)], axis=0)
        + jnp.concatenate([fetch(far_tile, far_source(part, True)) for part in (0, 1)], axis=0).T
    )
    even = [jnp.where(core == half, own, far_whole) for half in (0, 1)]
    return jnp.concatenate(
        [jnp.where(xh == xl, even[half], near_tiles[half]) for half in (0, 1)], axis=1
    )


def solution(mesh):
    fine = Mesh(mesh.devices.reshape(SIZES), AXES)
    return jax.shard_map(
        body,
        mesh=fine,
        in_specs=(P(AXES, None), P(AXES), P(AXES), P(), P(), P(), P()),
        out_specs=P(("xh", "y", "core"), ("xl", "z")),
        check_vma=False,
    )
```

```python
import functools

import jax
import jax.numpy as jnp
from jax import lax
from jax.experimental import pallas as pl
from jax.experimental.pallas import tpu as pltpu
from jax.sharding import Mesh, PartitionSpec as P

AXES = ("xl", "z", "xh", "y", "core")
SIZES = (2, 4, 2, 4, 2)
PLANE = ("z", "y", "core")
RING = ("xl", "xh", "core")
CHUNKS = 2
INTERPRET = False


def row_weights(row_period, row_site, period_err, site_err):
    period_hit = row_period[:, None] == jnp.arange(period_err.shape[0], dtype=jnp.int32)[None, :]
    site_hit = row_site[:, None] == jnp.arange(site_err.shape[0], dtype=jnp.int32)[None, :]
    period_scale = jnp.sum(jnp.where(period_hit, period_err[None, :], 0.0), axis=1)
    site_scale = jnp.sum(jnp.where(site_hit, site_err[None, :], 0.0), axis=1)
    return 1.0 / jnp.sqrt(period_scale * period_scale + site_scale * site_scale)


def flat(xl, z, xh, y, core):
    return (((xl * 4 + z) * 2 + xh) * 4 + y) * 2 + core


def ring_index(x, core):
    return ((x % 2) * 2 + x // 2) * 2 + core


def to_ring_neighbour():
    pairs = []
    for x in range(4):
        pairs.append((ring_index((x + 1) % 4, 0), ring_index(x, 0)))
        pairs.append((ring_index((x - 1) % 4, 1), ring_index(x, 1)))
    return pairs


def plane_shift(shift, first):
    pairs = []
    for z in range(4):
        for y in range(4):
            for core in range(2):
                along_y = (core == 0) == first
                to_z, to_y = (z, (y + shift) % 4) if along_y else ((z + shift) % 4, y)
                pairs.append(((z * 4 + y) * 2 + core, (to_z * 4 + to_y) * 2 + core))
    return pairs


def homes(place):
    pairs = []
    for xl in range(2):
        for z in range(4):
            for xh in range(2):
                for y in range(4):
                    for core in range(2):
                        source = place(xl, z, xh, y, core)
                        if source is not None:
                            pairs.append((flat(*source), flat(xl, z, xh, y, core)))
    return pairs


def near_source(half, mirrored):
    def place(xl, z, xh, y, core):
        if xh == xl:
            return None
        forward = (2 * core + xh - (2 * half + xl)) % 4 == 1
        holder = 0 if forward else 1
        if mirrored:
            return (xh, y, core, z, 1 - holder)
        return (xl, z, half, y, holder)

    return place


def own_source(part):
    return lambda xl, z, xh, y, core: (xl, z, core, y, part) if xh == xl else None


def far_source(part, mirrored):
    def place(xl, z, xh, y, core):
        if xh != xl:
            return None
        return (xl, y, core, z, part) if mirrored else (xl, z, 1 - core, y, part)

    return place


def tile_kernel(scal_ref, *refs, chunks, n_out):
    lhs, rhs = refs[:chunks], refs[chunks : 2 * chunks]
    outs, scratch = refs[2 * chunks : 2 * chunks + n_out], refs[-1]
    c = pl.program_id(0)
    height, tile = scratch.shape[2:]
    total = None
    for a, b in zip(lhs, rhs):
        part = lax.dot_general(
            a[...].reshape(4 * height, a.shape[-1]),
            b[...],
            (((1,), (1,)), ((), ())),
            preferred_element_type=jnp.float32,
        )
        total = part if total is None else total + part
    across = lax.rem(c + 4 - scal_ref[1], 4)
    for r in range(4):
        down = lax.rem(r + 4 - scal_ref[0], 4)
        s = jnp.where(scal_ref[2] == 0, down, across)
        v = jnp.where(scal_ref[2] == 0, across, down)
        scratch[s, v] = total[r * height : (r + 1) * height]

    @pl.when(c == 3)
    def _():
        if n_out == 1:
            outs[0][...] = scratch[...]
        else:
            for i in range(4):
                outs[i][...] = scratch[i]

def tile_products(lhs, rhs, scalars, split, joined, windowed):
    rows, depth = lhs[0].shape
    tile = rows // 4
    height = tile // 2 if split else tile
    chunks = len(lhs)
    lhs = [a.reshape(4, tile // height, height, depth) for a in lhs]
    if joined:
        out_shape = [jax.ShapeDtypeStruct((4, 4, height, tile), jnp.float32)]
        out_specs = [pl.BlockSpec((4, 4, height, tile), lambda c, scal: (0, 0, 0, 0))]
    else:
        out_shape = [jax.ShapeDtypeStruct((4, height, tile), jnp.float32)] * 4
        out_specs = [pl.BlockSpec((4, height, tile), lambda c, scal: (0, 0, 0))] * 4
    return pl.pallas_call(
        functools.partial(tile_kernel, chunks=chunks, n_out=len(out_shape)),
        out_shape=out_shape,
        grid_spec=pltpu.PrefetchScalarGridSpec(
            num_scalar_prefetch=1,
            grid=(4,),
            in_specs=[
                pl.BlockSpec(
                    (4, 1, height, depth),
                    lambda c, scal: (0, scal[3], 0, 0),
                    pipeline_mode=pl.Buffered(1),
                )
            ]
            * chunks
            + [pl.BlockSpec((tile, depth), lambda c, scal: (c, scal[4] if windowed else 0))] * chunks,
            out_specs=out_specs,
            scratch_shapes=[pltpu.VMEM((4, 4, height, tile), jnp.float32)],
        ),
        compiler_params=pltpu.CompilerParams(dimension_semantics=("arbitrary",), vmem_limit_bytes=48 * 2**20),
        cost_estimate=pl.CostEstimate(
            flops=2 * 16 * height * tile * depth * chunks,
            bytes_accessed=16 * height * tile * 4 + chunks * (height * 4 + rows) * depth * 2,
            transcendentals=0,
        ),
        interpret=INTERPRET,
    )(scalars, *lhs, *rhs)


def reduce_plane(strips):
    total = strips[0]
    for shift in (1, 3, 2):
        total = total + lax.ppermute(strips[shift], PLANE, plane_shift(shift, True))
    tile = total[0]
    for shift in (1, 3, 2):
        tile = tile + lax.ppermute(total[shift], PLANE, plane_shift(shift, False))
    return tile


def swap_cores(value):
    return lax.ppermute(value, "core", [(0, 1), (1, 0)])


def body(sensitivity, row_period, row_site, period_err, site_err, cell_var, cell_perm):
    xl, z, xh, y, core = (lax.axis_index(name).astype(jnp.int32) for name in AXES)
    x = 2 * xh + xl
    cells = cell_var.shape[0]
    chunk = cells // CHUNKS
    depth = chunk // 32
    weight = row_weights(row_period, row_site, period_err, site_err)[:, None]

    first = ((z * 4 + y) * 2 + core) * depth
    positions = jnp.concatenate(
        [lax.dynamic_slice_in_dim(cell_perm, j * chunk + first, depth) for j in range(CHUNKS)]
    )
    column_var = cell_var[positions]

    scaled = []
    for j in range(CHUNKS):
        packed = (weight * sensitivity[:, j * chunk : (j + 1) * chunk]).astype(jnp.bfloat16)
        if j + 1 < CHUNKS:
            weight, packed = lax.optimization_barrier((weight, packed))
        else:
            packed, column_var = lax.optimization_barrier((packed, column_var))
        scaled.append(lax.all_to_all(packed, PLANE, split_axis=1, concat_axis=0, tiled=True))

    weighted = [
        (scaled[j].astype(jnp.float32) * column_var[None, j * depth : (j + 1) * depth]).astype(
            jnp.bfloat16
        )
        for j in range(CHUNKS)
    ]

    near = [lax.ppermute(part, RING, to_ring_neighbour()) for part in scaled]
    window = x // 2
    target = lax.rem(x + jnp.where(core == 0, 3, 1), 4)
    far = [
        lax.ppermute(
            lax.dynamic_slice_in_dim(part, (target // 2) * (depth // 2), depth // 2, 1),
            RING,
            to_ring_neighbour(),
        )
        for part in near
    ]

    def scalars(order, half):
        return jnp.stack([y, z, order, half, window]).astype(jnp.int32)

    def halves(lhs, windowed):
        sent = tile_products(lhs, weighted, scalars(1 - core, 1 - core), True, True, windowed)[0]
        kept = tile_products(lhs, weighted, scalars(core, core), True, False, windowed)
        got = swap_cores(sent)
        return reduce_plane([kept[s] + got[s] for s in range(4)])

    own_tile = halves(scaled, False)
    near_tile = reduce_plane(tile_products(near, weighted, scalars(core, 0 * core), False, False, False))
    far_tile = halves(far, True)

    def fetch(value, place):
        return lax.ppermute(value, AXES, homes(place))

    own = jnp.concatenate([fetch(own_tile, own_source(part)) for part in (0, 1)], axis=0)
    near_tiles = [
        fetch(near_tile, near_source(half, False)) + fetch(near_tile, near_source(half, True)).T
        for half in (0, 1)
    ]
    far_whole = (
        jnp.concatenate([fetch(far_tile, far_source(part, False)) for part in (0, 1)], axis=0)
        + jnp.concatenate([fetch(far_tile, far_source(part, True)) for part in (0, 1)], axis=0).T
    )
    even = [jnp.where(core == half, own, far_whole) for half in (0, 1)]
    return jnp.concatenate(
        [jnp.where(xh == xl, even[half], near_tiles[half]) for half in (0, 1)], axis=1
    )


def solution(mesh):
    fine = Mesh(mesh.devices.reshape(SIZES), AXES)
    return jax.shard_map(
        body,
        mesh=fine,
        in_specs=(P(AXES, None), P(AXES), P(AXES), P(), P(), P(), P()),
        out_specs=P(("xh", "y", "core"), ("xl", "z")),
        check_vma=False,
    )
```

```python
import functools

import jax
import jax.numpy as jnp
from jax import lax
from jax.experimental import pallas as pl
from jax.experimental.pallas import tpu as pltpu
from jax.sharding import Mesh, PartitionSpec as P


AXES = ("xl", "z", "xh", "y", "core")
SIZES = (2, 4, 2, 4, 2)
PLANE = ("z", "y", "core")
RING = ("xl", "xh", "core")
CHUNKS = 2
INTERPRET = False


def row_weights(row_period, row_site, period_err, site_err):
    period_hit = row_period[:, None] == jnp.arange(period_err.shape[0], dtype=jnp.int32)[None, :]
    site_hit = row_site[:, None] == jnp.arange(site_err.shape[0], dtype=jnp.int32)[None, :]
    period_scale = jnp.sum(jnp.where(period_hit, period_err[None, :], 0.0), axis=1)
    site_scale = jnp.sum(jnp.where(site_hit, site_err[None, :], 0.0), axis=1)
    return 1.0 / jnp.sqrt(period_scale * period_scale + site_scale * site_scale)


def flat(xl, z, xh, y, core):
    return (((xl * 4 + z) * 2 + xh) * 4 + y) * 2 + core


def ring_index(x, core):
    return ((x % 2) * 2 + x // 2) * 2 + core


def to_ring_neighbour():
    pairs = []
    for x in range(4):
        pairs.append((ring_index((x + 1) % 4, 0), ring_index(x, 0)))
        pairs.append((ring_index((x - 1) % 4, 1), ring_index(x, 1)))
    return pairs


def plane_shift(shift, first):
    pairs = []
    for z in range(4):
        for y in range(4):
            for core in range(2):
                along_y = (core == 0) == first
                to_z, to_y = (z, (y + shift) % 4) if along_y else ((z + shift) % 4, y)
                pairs.append(((z * 4 + y) * 2 + core, (to_z * 4 + to_y) * 2 + core))
    return pairs


def homes(place):
    pairs = []
    for xl in range(2):
        for z in range(4):
            for xh in range(2):
                for y in range(4):
                    for core in range(2):
                        source = place(xl, z, xh, y, core)
                        if source is not None:
                            pairs.append((flat(*source), flat(xl, z, xh, y, core)))
    return pairs


def near_source(half, mirrored):
    def place(xl, z, xh, y, core):
        if xh == xl:
            return None
        forward = (2 * core + xh - (2 * half + xl)) % 4 == 1
        holder = 0 if forward else 1
        if mirrored:
            return (xh, y, core, z, 1 - holder)
        return (xl, z, half, y, holder)

    return place


def own_source(part):
    return lambda xl, z, xh, y, core: (xl, z, core, y, part) if xh == xl else None


def far_source(part, mirrored):
    def place(xl, z, xh, y, core):
        if xh != xl:
            return None
        return (xl, y, core, z, part) if mirrored else (xl, z, 1 - core, y, part)

    return place


def tile_kernel(scal_ref, *refs, chunks, n_out):
    lhs, rhs = refs[:chunks], refs[chunks : 2 * chunks]
    outs, scratch = refs[2 * chunks : 2 * chunks + n_out], refs[-1]
    c = pl.program_id(0)
    height, _ = scratch.shape[2:]
    total = None
    for a, b in zip(lhs, rhs):
        part = lax.dot_general(
            a[...].reshape(4 * height, a.shape[-1]),
            b[...],
            (((1,), (1,)), ((), ())),
            preferred_element_type=jnp.float32,
        )
        total = part if total is None else total + part
    across = lax.rem(c + 4 - scal_ref[1], 4)
    for r in range(4):
        down = lax.rem(r + 4 - scal_ref[0], 4)
        s = jnp.where(scal_ref[2] == 0, down, across)
        v = jnp.where(scal_ref[2] == 0, across, down)
        scratch[s, v] = total[r * height : (r + 1) * height]

    @pl.when(c == 3)
    def _():
        if n_out == 1:
            outs[0][...] = scratch[...]
        else:
            for i in range(4):
                outs[i][...] = scratch[i]


def tile_products(lhs, rhs, scalars, split, joined, windowed):
    rows, depth = lhs[0].shape
    tile = rows // 4
    height = tile // 2 if split else tile
    chunks = len(lhs)
    lhs = [a.reshape(4, tile // height, height, depth) for a in lhs]
    if joined:
        out_shape = [jax.ShapeDtypeStruct((4, 4, height, tile), jnp.float32)]
        out_specs = [pl.BlockSpec((4, 4, height, tile), lambda c, scal: (0, 0, 0, 0))]
    else:
        out_shape = [jax.ShapeDtypeStruct((4, height, tile), jnp.float32)] * 4
        out_specs = [pl.BlockSpec((4, height, tile), lambda c, scal: (0, 0, 0))] * 4
    return pl.pallas_call(
        functools.partial(tile_kernel, chunks=chunks, n_out=len(out_shape)),
        out_shape=out_shape,
        grid_spec=pltpu.PrefetchScalarGridSpec(
            num_scalar_prefetch=1,
            grid=(4,),
            in_specs=[
                pl.BlockSpec(
                    (4, 1, height, depth),
                    lambda c, scal: (0, scal[3], 0, 0),
                    pipeline_mode=pl.Buffered(1),
                )
            ]
            * chunks
            + [pl.BlockSpec((tile, depth), lambda c, scal: (c, scal[4] if windowed else 0))] * chunks,
            out_specs=out_specs,
            scratch_shapes=[pltpu.VMEM((4, 4, height, tile), jnp.float32)],
        ),
        compiler_params=pltpu.CompilerParams(dimension_semantics=("arbitrary",), vmem_limit_bytes=(14 if split else 24) * 2**20),
        cost_estimate=pl.CostEstimate(
            flops=2 * 16 * height * tile * depth * chunks,
            bytes_accessed=16 * height * tile * 4 + chunks * (height * 4 + rows) * depth * 2,
            transcendentals=0,
        ),
        interpret=INTERPRET,
    )(scalars, *lhs, *rhs)


def reduce_plane(strips):
    total = strips[0]
    for shift in (1, 3, 2):
        total = total + lax.ppermute(strips[shift], PLANE, plane_shift(shift, True))
    tile = total[0]
    for shift in (1, 3, 2):
        tile = tile + lax.ppermute(total[shift], PLANE, plane_shift(shift, False))
    return tile


def swap_cores(value):
    return lax.ppermute(value, "core", [(0, 1), (1, 0)])


def finish_kernel(scal_ref, *refs):
    near, own, far, out = refs[:4], refs[4:6], refs[6:10], refs[10]
    height, tile = own[0].shape

    @pl.when(scal_ref[0] == 0)
    def _():
        for half in range(2):
            out[:, half * tile : (half + 1) * tile] = near[2 * half][...] + near[2 * half + 1][...].T

    for half in range(2):

        @pl.when((scal_ref[0] == 1) & (scal_ref[1] == half))
        def _(half=half):
            other = (1 - half) * tile
            for part in range(2):
                rows = slice(part * height, (part + 1) * height)
                out[rows, half * tile : (half + 1) * tile] = own[part][...]
                mirrored = jnp.concatenate(
                    [far[2 + piece][:, rows].T for piece in range(2)], axis=1
                )
                out[rows, other : other + tile] = far[part][...] + mirrored


def finish(scalars, near, own, far):
    _, tile = own[0].shape
    operands = [*near, *own, *far]
    return pl.pallas_call(
        finish_kernel,
        out_shape=jax.ShapeDtypeStruct((tile, 2 * tile), jnp.float32),
        in_specs=[pl.BlockSpec(memory_space=pltpu.SMEM)]
        + [pl.BlockSpec(memory_space=pltpu.VMEM)] * len(operands),
        out_specs=pl.BlockSpec(memory_space=pltpu.VMEM),
        cost_estimate=pl.CostEstimate(
            flops=tile * tile * 2, bytes_accessed=tile * tile * 4 * 9, transcendentals=0
        ),
        interpret=INTERPRET,
    )(scalars, *operands)


def body(sensitivity, row_period, row_site, period_err, site_err, cell_var, cell_perm):
    xl, z, xh, y, core = (lax.axis_index(name).astype(jnp.int32) for name in AXES)
    x = 2 * xh + xl
    cells = cell_var.shape[0]
    chunk = cells // CHUNKS
    depth = chunk // 32
    weight = row_weights(row_period, row_site, period_err, site_err)[:, None]

    first = ((z * 4 + y) * 2 + core) * depth
    positions = jnp.concatenate([lax.dynamic_slice_in_dim(cell_perm, j * chunk + first, depth) for j in range(CHUNKS)])
    column_var = cell_var[positions]

    scaled = []
    for j in range(CHUNKS):
        packed = (weight * sensitivity[:, j * chunk : (j + 1) * chunk]).astype(jnp.bfloat16)
        if j + 1 < CHUNKS:
            weight, packed = lax.optimization_barrier((weight, packed))
        scaled.append(lax.all_to_all(packed, PLANE, split_axis=1, concat_axis=0, tiled=True))

    window = x // 2
    target = lax.rem(x + jnp.where(core == 0, 3, 1), 4)
    weighted, near, far = [], [], []
    for j in range(CHUNKS):
        near.append(lax.ppermute(scaled[j], RING, to_ring_neighbour()))
        var = column_var[None, j * depth : (j + 1) * depth]
        weighted.append((scaled[j].astype(jnp.float32) * var).astype(jnp.bfloat16))
        cut = lax.dynamic_slice_in_dim(near[j], (target // 2) * (depth // 2), depth // 2, 1)
        far.append(lax.ppermute(cut, RING, to_ring_neighbour()))

    def scalars(order, half):
        return jnp.stack([y, z, order, half, window]).astype(jnp.int32)

    def halves(lhs, windowed):
        sent = tile_products(lhs, weighted, scalars(1 - core, 1 - core), True, True, windowed)[0]
        got = swap_cores(sent)
        kept = tile_products(lhs, weighted, scalars(core, core), True, False, windowed)
        strips = [kept[s] + got[s] for s in range(4)]
        return reduce_plane(strips)

    own_tile = halves(scaled, False)
    strips = tile_products(near, weighted, scalars(core, 0 * core), False, False, False)
    near_tile = reduce_plane(strips)
    far_tile = halves(far, True)

    def fetch(value, place):
        return lax.ppermute(value, AXES, homes(place))

    own = [fetch(own_tile, own_source(part)) for part in (0, 1)]
    pair = [fetch(near_tile, near_source(half, mirrored)) for half in (0, 1) for mirrored in (False, True)]
    two = [fetch(far_tile, far_source(part, mirrored)) for mirrored in (False, True) for part in (0, 1)]
    return finish(jnp.stack([(xh == xl).astype(jnp.int32), core]), pair, own, two)


def solution(mesh):
    fine = Mesh(mesh.devices.reshape(SIZES), AXES)

    return jax.shard_map(
        body,
        mesh=fine,
        in_specs=(P(AXES, None), P(AXES), P(AXES), P(), P(), P(), P()),
        out_specs=P(("xh", "y", "core"), ("xl", "z")),
        check_vma=False,
    )
```

```python
import functools

import jax
import jax.numpy as jnp
from jax import lax
from jax.experimental import pallas as pl
from jax.experimental.pallas import tpu as pltpu
from jax.sharding import Mesh, PartitionSpec as P


AXES = ("xl", "z", "xh", "y", "core")
SIZES = (2, 4, 2, 4, 2)
PLANE = ("z", "y", "core")
RING = ("xl", "xh", "core")
PARTS = (5, 3)
CHUNKS = len(PARTS)
INTERPRET = False
VMEM_GRANT = 60 * 2**20


def row_weights(row_period, row_site, period_err, site_err):
    period_hit = row_period[:, None] == jnp.arange(period_err.shape[0], dtype=jnp.int32)[None, :]
    site_hit = row_site[:, None] == jnp.arange(site_err.shape[0], dtype=jnp.int32)[None, :]
    period_scale = jnp.sum(jnp.where(period_hit, period_err[None, :], 0.0), axis=1)
    site_scale = jnp.sum(jnp.where(site_hit, site_err[None, :], 0.0), axis=1)
    return 1.0 / jnp.sqrt(period_scale * period_scale + site_scale * site_scale)


def pack_kernel(period_ref, site_ref, period_err_ref, site_err_ref, data_ref, out_ref, weight_ref):
    rows = data_ref.shape[0]
    blocks, _, depth = out_ref.shape

    @pl.when(pl.program_id(0) == 0)
    def _():
        def iota(shape, axis):
            return lax.broadcasted_iota(jnp.int32, shape, axis)

        def looked_up(index_ref, table_ref):
            square = (rows, rows)
            diagonal = iota(square, 0) == iota(square, 1)
            index = jnp.sum(
                jnp.where(diagonal, index_ref[...].astype(jnp.float32), 0.0), axis=1, keepdims=True
            ).astype(jnp.int32)
            hit = index == iota((rows, table_ref.shape[1]), 1)
            return jnp.sum(jnp.where(hit, table_ref[...], 0.0), axis=1, keepdims=True)

        period_scale = looked_up(period_ref, period_err_ref)
        site_scale = looked_up(site_ref, site_err_ref)
        weight = 1.0 / jnp.sqrt(period_scale * period_scale + site_scale * site_scale)
        weight_ref[...] = jnp.broadcast_to(weight, weight_ref.shape)

    weight = weight_ref[:, :1]
    for block in range(blocks):
        data = data_ref[:, block * depth : (block + 1) * depth]
        out_ref[block] = (weight * data).astype(jnp.bfloat16)


def pack_first(sensitivity, row_period, row_site, period_err, site_err, depth):
    rows = sensitivity.shape[0]
    steps = 4
    tables = [a[None, :] for a in (row_period, row_site, period_err, site_err)]
    return pl.pallas_call(
        pack_kernel,
        out_shape=jax.ShapeDtypeStruct((32, rows, depth), jnp.bfloat16),
        grid=(steps,),
        in_specs=[pl.BlockSpec(a.shape, lambda i: (0, 0)) for a in tables]
        + [pl.BlockSpec((rows, 32 // steps * depth), lambda i: (0, i))],
        out_specs=pl.BlockSpec((32 // steps, rows, depth), lambda i: (i, 0, 0)),
        scratch_shapes=[pltpu.VMEM((rows, 128), jnp.float32)],
        compiler_params=pltpu.CompilerParams(
            dimension_semantics=("arbitrary",), vmem_limit_bytes=VMEM_GRANT
        ),
        cost_estimate=pl.CostEstimate(
            flops=32 * rows * depth, bytes_accessed=32 * rows * depth * 6, transcendentals=0
        ),
        interpret=INTERPRET,
    )(*tables, sensitivity)


def flat(xl, z, xh, y, core):
    return (((xl * 4 + z) * 2 + xh) * 4 + y) * 2 + core


def ring_index(x, core):
    return ((x % 2) * 2 + x // 2) * 2 + core


def to_ring_neighbour():
    pairs = []
    for x in range(4):
        pairs.append((ring_index((x + 1) % 4, 0), ring_index(x, 0)))
        pairs.append((ring_index((x - 1) % 4, 1), ring_index(x, 1)))
    return pairs


def plane_shift(shift, first):
    pairs = []
    for z in range(4):
        for y in range(4):
            for core in range(2):
                along_y = (core == 0) == first
                to_z, to_y = (z, (y + shift) % 4) if along_y else ((z + shift) % 4, y)
                pairs.append(((z * 4 + y) * 2 + core, (to_z * 4 + to_y) * 2 + core))
    return pairs


def homes(place):
    pairs = []
    for xl in range(2):
        for z in range(4):
            for xh in range(2):
                for y in range(4):
                    for core in range(2):
                        source = place(xl, z, xh, y, core)
                        if source is not None:
                            pairs.append((flat(*source), flat(xl, z, xh, y, core)))
    return pairs


def own_source(part):
    return lambda xl, z, xh, y, core: (xl, z, core, y, part) if xh == xl else None


def near_source(half, mirrored):
    def place(xl, z, xh, y, core):
        if xh == xl:
            return None
        forward = (2 * core + xh - (2 * half + xl)) % 4 == 1
        holder = 0 if forward else 1
        return (xh, y, core, z, 1 - holder) if mirrored else (xl, z, half, y, holder)

    return place


def far_source(half, mirrored):
    def place(xl, z, xh, y, core):
        if xh != xl:
            return None
        part, flip = far_role(xl, core, half, mirrored)
        return (xl, y, core, z, part) if flip else (xl, z, 1 - core, y, part)

    return place


def both(first, second):
    return lambda *device: first(*device) or second(*device)


def far_role(xl, core, half, mirrored):
    slot = (2 + (half ^ (1 - xl))) if mirrored else half
    return (((0, 0), (0, 1), (1, 0), (1, 1)), ((1, 1), (1, 0), (0, 0), (0, 1)))[core][slot]


def tile_kernel(scal_ref, *refs, chunks, n_out, based):
    lhs, rhs = refs[:chunks], refs[chunks : 2 * chunks]
    base = refs[2 * chunks] if based else None
    outs, scratch = refs[2 * chunks + based : 2 * chunks + based + n_out], refs[-1]
    c = pl.program_id(0)
    height, _ = scratch.shape[2:]
    total = None
    for a, b in zip(lhs, rhs):
        part = lax.dot_general(
            a[...].reshape(4 * height, a.shape[-1]),
            b[...],
            (((1,), (1,)), ((), ())),
            preferred_element_type=jnp.float32,
        )
        total = part if total is None else total + part
    across = lax.rem(c + 4 - scal_ref[1], 4)
    for r in range(4):
        down = lax.rem(r + 4 - scal_ref[0], 4)
        s = jnp.where(scal_ref[2] == 0, down, across)
        v = jnp.where(scal_ref[2] == 0, across, down)
        scratch[s, v] = total[r * height : (r + 1) * height]

    @pl.when(c == 3)
    def _():
        if n_out == 1:
            outs[0][...] = scratch[...]
        else:
            for i in range(4):
                outs[i][...] = scratch[i] + base[i] if based else scratch[i]


def tile_products(lhs, rhs, scalars, split=False, joined=False, windowed=False, base=None):
    rows = lhs[0].shape[0]
    depths = [a.shape[1] for a in lhs]
    tile = rows // 4
    height = tile // 2 if split else tile
    lhs = [a.reshape(4, tile // height, height, depth) for a, depth in zip(lhs, depths)]
    if joined:
        out_shape = [jax.ShapeDtypeStruct((4, 4, height, tile), jnp.float32)]
        out_specs = [pl.BlockSpec((4, 4, height, tile), lambda c, scal: (0, 0, 0, 0))]
    else:
        out_shape = [jax.ShapeDtypeStruct((4, height, tile), jnp.float32)] * 4
        out_specs = [pl.BlockSpec((4, height, tile), lambda c, scal: (0, 0, 0))] * 4
    lhs_specs = [
        pl.BlockSpec(
            (4, 1, height, depth),
            lambda c, scal: (0, scal[3], 0, 0),
            pipeline_mode=pl.Buffered(1),
        )
        for depth in depths
    ]
    rhs_specs = [
        pl.BlockSpec((tile, depth), lambda c, scal: (c, scal[4] if windowed else 0))
        for depth in depths
    ]
    extra = [] if base is None else [base]
    base_specs = [
        pl.BlockSpec(a.shape, lambda c, scal: (0, 0, 0, 0), pipeline_mode=pl.Buffered(1))
        for a in extra
    ]
    return pl.pallas_call(
        functools.partial(
            tile_kernel, chunks=len(lhs), n_out=len(out_shape), based=len(extra)
        ),
        out_shape=out_shape,
        grid_spec=pltpu.PrefetchScalarGridSpec(
            num_scalar_prefetch=1,
            grid=(4,),
            in_specs=lhs_specs + rhs_specs + base_specs,
            out_specs=out_specs,
            scratch_shapes=[pltpu.VMEM((4, 4, height, tile), jnp.float32)],
        ),
        compiler_params=pltpu.CompilerParams(
            dimension_semantics=("arbitrary",), vmem_limit_bytes=VMEM_GRANT
        ),
        cost_estimate=pl.CostEstimate(
            flops=2 * 16 * height * tile * sum(depths),
            bytes_accessed=16 * height * tile * 4 + (height * 4 + rows) * sum(depths) * 2,
            transcendentals=0,
        ),
        interpret=INTERPRET,
    )(scalars, *lhs, *rhs, *extra)


def reduce_plane(strips):
    total = strips[0]
    for shift in (1, 3, 2):
        total = total + lax.ppermute(strips[shift], PLANE, plane_shift(shift, True))
    tile = total[0]
    for shift in (1, 3, 2):
        tile = tile + lax.ppermute(total[shift], PLANE, plane_shift(shift, False))
    return tile


def swap_cores(value):
    return lax.ppermute(value, "core", [(0, 1), (1, 0)])


def finish_kernel(scal_ref, *refs):
    direct, mixed, far, own, out = refs[:2], refs[2:4], refs[4:6], refs[6:8], refs[8]
    height, tile = own[0].shape
    core, even, xl = scal_ref[2], scal_ref[5], scal_ref[6]

    @pl.when(even == 0)
    def _():
        for half in range(2):
            out[:, half * tile : (half + 1) * tile] = direct[half][...] + mixed[half][...].T

    for xl_at in range(2):
        for core_at in range(2):

            @pl.when((even == 1) & (xl == xl_at) & (core == core_at))
            def _(xl_at=xl_at, core_at=core_at):
                parts = {}
                for half in range(2):
                    parts[far_role(xl_at, core_at, half, 0)] = far[half]
                    parts[far_role(xl_at, core_at, half, 1)] = mixed[half]
                other = (1 - core_at) * tile
                for part in range(2):
                    rows = slice(part * height, (part + 1) * height)
                    out[rows, core_at * tile : (core_at + 1) * tile] = own[part][...]
                    mirrored = jnp.concatenate(
                        [parts[piece, 1][:height, rows].T for piece in range(2)], axis=1
                    )
                    out[rows, other : other + tile] = parts[part, 0][:height] + mirrored


def finish(scalars, *operands):
    tile = operands[0].shape[0]
    return pl.pallas_call(
        finish_kernel,
        out_shape=jax.ShapeDtypeStruct((tile, 2 * tile), jnp.float32),
        in_specs=[pl.BlockSpec(memory_space=pltpu.SMEM)]
        + [pl.BlockSpec(memory_space=pltpu.VMEM)] * len(operands),
        out_specs=pl.BlockSpec(memory_space=pltpu.VMEM),
        cost_estimate=pl.CostEstimate(
            flops=tile * tile * 2, bytes_accessed=tile * tile * 4 * 8, transcendentals=0
        ),
        interpret=INTERPRET,
    )(scalars, *operands)


def body(sensitivity, row_period, row_site, period_err, site_err, cell_var, cell_perm):
    xl, z, xh, y, core = (lax.axis_index(name).astype(jnp.int32) for name in AXES)
    x = 2 * xh + xl
    cells = cell_var.shape[0]
    rows = sensitivity.shape[0]
    depths = [cells // 32 * part // sum(PARTS) for part in PARTS]
    starts = [32 * sum(depths[:j]) for j in range(CHUNKS)]
    place = (z * 4 + y) * 2 + core
    positions = jnp.concatenate(
        [
            lax.dynamic_slice_in_dim(cell_perm, start + place * depth, depth)
            for start, depth in zip(starts, depths)
        ]
    )
    column_var = cell_var[positions]

    scaled = []
    for j, (start, depth) in enumerate(zip(starts, depths)):
        if j == 0:
            packed = pack_first(sensitivity, row_period, row_site, period_err, site_err, depth)
        else:
            weight = row_weights(row_period, row_site, period_err, site_err)[:, None]
            packed = (weight * sensitivity[:, start : start + 32 * depth]).astype(jnp.bfloat16)
            packed = packed.reshape(rows, 32, depth).transpose(1, 0, 2)
        moved = lax.all_to_all(packed, PLANE, split_axis=0, concat_axis=0, tiled=True)
        scaled.append(moved.reshape(32 * rows, depth))

    other_var = swap_cores(column_var)

    def weigh(rows_on_cells, var, j):
        piece = var[None, starts[j] // 32 : starts[j] // 32 + depths[j]]
        return (rows_on_cells.astype(jnp.float32) * piece).astype(jnp.bfloat16)

    window = x // 2
    target = lax.rem(x + jnp.where(core == 0, 3, 1), 4)
    weighted, near, far = [], [], []
    other, other_weighted, other_far = [], [], []
    for j, depth in enumerate(depths):
        near.append(lax.ppermute(scaled[j], RING, to_ring_neighbour()))
        other.append(swap_cores(scaled[j]))
        weighted.append(weigh(scaled[j], column_var, j))
        other_weighted.append(weigh(other[j], other_var, j))
        cut = lax.dynamic_slice_in_dim(near[j], (target // 2) * (depth // 2), depth // 2, 1)
        far.append(lax.ppermute(cut, RING, to_ring_neighbour()))
        other_far.append(swap_cores(far[j]))

    whole = jnp.stack([y, z, core, 0 * core, window, (xh == xl).astype(jnp.int32), xl])
    halved = jnp.stack([y, z, core, core, window])
    base = tile_products(
        [scaled[0], other[0]], [weighted[0], other_weighted[0]], halved, split=True, joined=True
    )[0]
    strips = tile_products(
        [scaled[1], other[1]], [weighted[1], other_weighted[1]], halved, split=True, base=base
    )
    own_tile = reduce_plane(strips)
    strips = tile_products(near, weighted, whole)
    near_tile = reduce_plane(strips)
    strips = tile_products(
        far + other_far, weighted + other_weighted, halved, split=True, windowed=True
    )
    far_tile = reduce_plane(strips)

    def fetch(value, place):
        return lax.ppermute(value, AXES, homes(place))

    own = [fetch(own_tile, own_source(part)) for part in (0, 1)]
    direct = [fetch(near_tile, near_source(half, False)) for half in (0, 1)]
    padded = jnp.concatenate([far_tile, far_tile], axis=0)
    odd = xl ^ xh ^ core
    chosen = [jnp.where(odd == half, near_tile, padded) for half in (0, 1)]
    mixed = [
        fetch(chosen[half], both(near_source(half, True), far_source(half, 1)))
        for half in (0, 1)
    ]
    two = [fetch(far_tile, far_source(half, 0)) for half in (0, 1)]
    return finish(whole, *direct, *mixed, *two, *own)


def solution(mesh):
    fine = Mesh(mesh.devices.reshape(SIZES), AXES)

    return jax.shard_map(
        body,
        mesh=fine,
        in_specs=(P(AXES, None), P(AXES), P(AXES), P(), P(), P(), P()),
        out_specs=P(("xh", "y", "core"), ("xl", "z")),
        check_vma=False,
    )
```

```python
import functools

import jax
import jax.numpy as jnp
from jax import lax
from jax.experimental import pallas as pl
from jax.experimental.pallas import tpu as pltpu
from jax.sharding import Mesh, PartitionSpec as P


AXES = ("xl", "z", "xh", "y", "core")
SIZES = (2, 4, 2, 4, 2)
PLANE = ("z", "y", "core")
RING = ("xl", "xh", "core")
PARTS = (5, 3)
CHUNKS = len(PARTS)
INTERPRET = False
VMEM_GRANT = 60 * 2**20
TILE_STEPS = 2


def row_weights(row_period, row_site, period_err, site_err):
    period_hit = row_period[:, None] == jnp.arange(period_err.shape[0], dtype=jnp.int32)[None, :]
    site_hit = row_site[:, None] == jnp.arange(site_err.shape[0], dtype=jnp.int32)[None, :]
    period_scale = jnp.sum(jnp.where(period_hit, period_err[None, :], 0.0), axis=1)
    site_scale = jnp.sum(jnp.where(site_hit, site_err[None, :], 0.0), axis=1)
    return 1.0 / jnp.sqrt(period_scale * period_scale + site_scale * site_scale)


def pack_kernel(period_ref, site_ref, period_err_ref, site_err_ref, data_ref, out_ref, weight_ref):
    rows = data_ref.shape[0]
    blocks, _, depth = out_ref.shape

    @pl.when(pl.program_id(0) == 0)
    def _():
        def iota(shape, axis):
            return lax.broadcasted_iota(jnp.int32, shape, axis)

        def looked_up(index_ref, table_ref):
            square = (rows, rows)
            diagonal = iota(square, 0) == iota(square, 1)
            index = jnp.sum(
                jnp.where(diagonal, index_ref[...].astype(jnp.float32), 0.0), axis=1, keepdims=True
            ).astype(jnp.int32)
            hit = index == iota((rows, table_ref.shape[1]), 1)
            return jnp.sum(jnp.where(hit, table_ref[...], 0.0), axis=1, keepdims=True)

        period_scale = looked_up(period_ref, period_err_ref)
        site_scale = looked_up(site_ref, site_err_ref)
        weight = 1.0 / jnp.sqrt(period_scale * period_scale + site_scale * site_scale)
        weight_ref[...] = jnp.broadcast_to(weight, weight_ref.shape)

    weight = weight_ref[:, :1]
    for block in range(blocks):
        data = data_ref[:, block * depth : (block + 1) * depth]
        out_ref[block] = (weight * data).astype(jnp.bfloat16)


def pack_first(sensitivity, row_period, row_site, period_err, site_err, depth):
    rows = sensitivity.shape[0]
    steps = 2
    tables = [a[None, :] for a in (row_period, row_site, period_err, site_err)]
    return pl.pallas_call(
        pack_kernel,
        out_shape=jax.ShapeDtypeStruct((32, rows, depth), jnp.bfloat16),
        grid=(steps,),
        in_specs=[pl.BlockSpec(a.shape, lambda i: (0, 0)) for a in tables]
        + [pl.BlockSpec((rows, 32 // steps * depth), lambda i: (0, i))],
        out_specs=pl.BlockSpec((32 // steps, rows, depth), lambda i: (i, 0, 0)),
        scratch_shapes=[pltpu.VMEM((rows, 128), jnp.float32)],
        compiler_params=pltpu.CompilerParams(
            dimension_semantics=("arbitrary",), vmem_limit_bytes=VMEM_GRANT
        ),
        cost_estimate=pl.CostEstimate(
            flops=32 * rows * depth, bytes_accessed=32 * rows * depth * 6, transcendentals=0
        ),
        interpret=INTERPRET,
    )(*tables, sensitivity)


def flat(xl, z, xh, y, core):
    return (((xl * 4 + z) * 2 + xh) * 4 + y) * 2 + core


def ring_index(x, core):
    return ((x % 2) * 2 + x // 2) * 2 + core


def to_ring_neighbour():
    pairs = []
    for x in range(4):
        pairs.append((ring_index((x + 1) % 4, 0), ring_index(x, 0)))
        pairs.append((ring_index((x - 1) % 4, 1), ring_index(x, 1)))
    return pairs


def plane_shift(shift, first):
    pairs = []
    for z in range(4):
        for y in range(4):
            for core in range(2):
                along_y = (core == 0) == first
                to_z, to_y = (z, (y + shift) % 4) if along_y else ((z + shift) % 4, y)
                pairs.append(((z * 4 + y) * 2 + core, (to_z * 4 + to_y) * 2 + core))
    return pairs


def homes(place):
    pairs = []
    for xl in range(2):
        for z in range(4):
            for xh in range(2):
                for y in range(4):
                    for core in range(2):
                        source = place(xl, z, xh, y, core)
                        if source is not None:
                            pairs.append((flat(*source), flat(xl, z, xh, y, core)))
    return pairs


def own_source(part):
    return lambda xl, z, xh, y, core: (xl, z, core, y, part) if xh == xl else None


def near_source(half, mirrored):
    def place(xl, z, xh, y, core):
        if xh == xl:
            return None
        forward = (2 * core + xh - (2 * half + xl)) % 4 == 1
        holder = 0 if forward else 1
        return (xh, y, core, z, 1 - holder) if mirrored else (xl, z, half, y, holder)

    return place


def far_source(half, mirrored):
    def place(xl, z, xh, y, core):
        if xh != xl:
            return None
        part, flip = far_role(xl, core, half, mirrored)
        return (xl, y, core, z, part) if flip else (xl, z, 1 - core, y, part)

    return place


def both(first, second):
    return lambda *device: first(*device) or second(*device)


def far_role(xl, core, half, mirrored):
    slot = (2 + (half ^ (1 - xl))) if mirrored else half
    return (((0, 0), (0, 1), (1, 0), (1, 1)), ((1, 1), (1, 0), (0, 0), (0, 1)))[core][slot]


def tile_kernel(scal_ref, *refs, chunks, n_out, based):
    lhs, rhs = refs[:chunks], refs[chunks : 2 * chunks]
    base = refs[2 * chunks] if based else None
    outs, scratch = refs[2 * chunks + based : 2 * chunks + based + n_out], refs[-1]
    c = pl.program_id(0)
    height, tile = scratch.shape[2:]
    columns = 4 // TILE_STEPS
    total = None
    for a, b in zip(lhs, rhs):
        part = lax.dot_general(
            a[...].reshape(4 * height, a.shape[-1]),
            b[...],
            (((1,), (1,)), ((), ())),
            preferred_element_type=jnp.float32,
        )
        total = part if total is None else total + part
    for column in range(columns):
        across = lax.rem(c * columns + column + 4 - scal_ref[1], 4)
        for r in range(4):
            down = lax.rem(r + 4 - scal_ref[0], 4)
            s = jnp.where(scal_ref[2] == 0, down, across)
            v = jnp.where(scal_ref[2] == 0, across, down)
            scratch[s, v] = total[
                r * height : (r + 1) * height, column * tile : (column + 1) * tile
            ]

    @pl.when(c == TILE_STEPS - 1)
    def _():
        if n_out == 1:
            outs[0][...] = scratch[...]
        else:
            for i in range(4):
                outs[i][...] = scratch[i] + base[i] if based else scratch[i]


def tile_products(lhs, rhs, scalars, split=False, joined=False, windowed=False, base=None):
    rows = lhs[0].shape[0]
    depths = [a.shape[1] for a in lhs]
    tile = rows // 4
    height = tile // 2 if split else tile
    lhs = [a.reshape(4, tile // height, height, depth) for a, depth in zip(lhs, depths)]
    if joined:
        out_shape = [jax.ShapeDtypeStruct((4, 4, height, tile), jnp.float32)]
        out_specs = [pl.BlockSpec((4, 4, height, tile), lambda c, scal: (0, 0, 0, 0))]
    else:
        out_shape = [jax.ShapeDtypeStruct((4, height, tile), jnp.float32)] * 4
        out_specs = [pl.BlockSpec((4, height, tile), lambda c, scal: (0, 0, 0))] * 4
    lhs_specs = [
        pl.BlockSpec(
            (4, 1, height, depth),
            lambda c, scal: (0, scal[3], 0, 0),
            pipeline_mode=pl.Buffered(1),
        )
        for depth in depths
    ]
    rhs_specs = [
        pl.BlockSpec((rows // TILE_STEPS, depth), lambda c, scal: (c, scal[4] if windowed else 0))
        for depth in depths
    ]
    extra = [] if base is None else [base]
    base_specs = [
        pl.BlockSpec(a.shape, lambda c, scal: (0, 0, 0, 0), pipeline_mode=pl.Buffered(1))
        for a in extra
    ]
    return pl.pallas_call(
        functools.partial(
            tile_kernel, chunks=len(lhs), n_out=len(out_shape), based=len(extra)
        ),
        out_shape=out_shape,
        grid_spec=pltpu.PrefetchScalarGridSpec(
            num_scalar_prefetch=1,
            grid=(TILE_STEPS,),
            in_specs=lhs_specs + rhs_specs + base_specs,
            out_specs=out_specs,
            scratch_shapes=[pltpu.VMEM((4, 4, height, tile), jnp.float32)],
        ),
        compiler_params=pltpu.CompilerParams(
            dimension_semantics=("arbitrary",), vmem_limit_bytes=VMEM_GRANT
        ),
        cost_estimate=pl.CostEstimate(
            flops=2 * 16 * height * tile * sum(depths),
            bytes_accessed=16 * height * tile * 4 + (height * 4 + rows) * sum(depths) * 2,
            transcendentals=0,
        ),
        interpret=INTERPRET,
    )(scalars, *lhs, *rhs, *extra)


def reduce_first(strips):
    total = strips[0]
    for shift in (1, 3, 2):
        total = total + lax.ppermute(strips[shift], PLANE, plane_shift(shift, True))
    return total


def reduce_second(totals):
    heights = [total.shape[1] for total in totals]
    total = jnp.concatenate(totals, axis=1) if len(totals) > 1 else totals[0]
    tile = total[0]
    for shift in (1, 3, 2):
        tile = tile + lax.ppermute(total[shift], PLANE, plane_shift(shift, False))
    tiles, row = [], 0
    for height in heights:
        tiles.append(tile[row : row + height])
        row += height
    return tiles


def swap_cores(value):
    return lax.ppermute(value, "core", [(0, 1), (1, 0)])


def finish_kernel(scal_ref, *refs):
    direct, mixed, far, own, out = refs[:2], refs[2:4], refs[4:6], refs[6:8], refs[8]
    height, tile = own[0].shape
    core, even, xl = scal_ref[2], scal_ref[5], scal_ref[6]

    @pl.when(even == 0)
    def _():
        for half in range(2):
            out[:, half * tile : (half + 1) * tile] = direct[half][...] + mixed[half][...].T

    for xl_at in range(2):
        for core_at in range(2):

            @pl.when((even == 1) & (xl == xl_at) & (core == core_at))
            def _(xl_at=xl_at, core_at=core_at):
                parts = {}
                for half in range(2):
                    parts[far_role(xl_at, core_at, half, 0)] = far[half]
                    parts[far_role(xl_at, core_at, half, 1)] = mixed[half]
                other = (1 - core_at) * tile
                for part in range(2):
                    rows = slice(part * height, (part + 1) * height)
                    out[rows, core_at * tile : (core_at + 1) * tile] = own[part][...]
                    mirrored = jnp.concatenate(
                        [parts[piece, 1][:height, rows].T for piece in range(2)], axis=1
                    )
                    out[rows, other : other + tile] = parts[part, 0][:height] + mirrored


def finish(scalars, *operands):
    tile = operands[0].shape[0]
    return pl.pallas_call(
        finish_kernel,
        out_shape=jax.ShapeDtypeStruct((tile, 2 * tile), jnp.float32),
        in_specs=[pl.BlockSpec(memory_space=pltpu.SMEM)]
        + [pl.BlockSpec(memory_space=pltpu.VMEM)] * len(operands),
        out_specs=pl.BlockSpec(memory_space=pltpu.VMEM),
        cost_estimate=pl.CostEstimate(
            flops=tile * tile * 2, bytes_accessed=tile * tile * 4 * 8, transcendentals=0
        ),
        compiler_params=pltpu.CompilerParams(vmem_limit_bytes=6 * 2**20),
        interpret=INTERPRET,
    )(scalars, *operands)


def body(sensitivity, row_period, row_site, period_err, site_err, cell_var, cell_perm):
    xl, z, xh, y, core = (lax.axis_index(name).astype(jnp.int32) for name in AXES)
    x = 2 * xh + xl
    cells = cell_var.shape[0]
    rows = sensitivity.shape[0]
    depths = [cells // 32 * part // sum(PARTS) for part in PARTS]
    starts = [32 * sum(depths[:j]) for j in range(CHUNKS)]
    place = (z * 4 + y) * 2 + core
    positions = jnp.concatenate(
        [
            lax.dynamic_slice_in_dim(cell_perm, start + place * depth, depth)
            for start, depth in zip(starts, depths)
        ]
    )
    column_var = cell_var[positions]

    scaled = []
    for j, (start, depth) in enumerate(zip(starts, depths)):
        if j == 0:
            packed = pack_first(sensitivity, row_period, row_site, period_err, site_err, depth)
        else:
            weight = row_weights(row_period, row_site, period_err, site_err)[:, None]
            packed = (weight * sensitivity[:, start : start + 32 * depth]).astype(jnp.bfloat16)
            packed = packed.reshape(rows, 32, depth).transpose(1, 0, 2)
        moved = lax.all_to_all(packed, PLANE, split_axis=0, concat_axis=0, tiled=True)
        scaled.append(moved.reshape(32 * rows, depth))

    other_var = swap_cores(column_var)

    def weigh(rows_on_cells, var, j):
        piece = var[None, starts[j] // 32 : starts[j] // 32 + depths[j]]
        return (rows_on_cells.astype(jnp.float32) * piece).astype(jnp.bfloat16)

    window = x // 2
    target = lax.rem(x + jnp.where(core == 0, 3, 1), 4)
    weighted, near, far = [], [], []
    other, other_weighted, other_far = [], [], []
    for j, depth in enumerate(depths):
        near.append(lax.ppermute(scaled[j], RING, to_ring_neighbour()))
        other.append(swap_cores(scaled[j]))
        weighted.append(weigh(scaled[j], column_var, j))
        other_weighted.append(weigh(other[j], other_var, j))
        cut = lax.dynamic_slice_in_dim(near[j], (target // 2) * (depth // 2), depth // 2, 1)
        far.append(lax.ppermute(cut, RING, to_ring_neighbour()))
        other_far.append(swap_cores(far[j]))

    whole = jnp.stack([y, z, core, 0 * core, window, (xh == xl).astype(jnp.int32), xl])
    halved = jnp.stack([y, z, core, core, window])
    base = tile_products(
        [scaled[0], other[0]], [weighted[0], other_weighted[0]], halved, split=True, joined=True
    )[0]
    strips = tile_products(
        [scaled[1], other[1]], [weighted[1], other_weighted[1]], halved, split=True, base=base
    )
    own_total = reduce_first(strips)
    strips = tile_products(near, weighted, whole)
    near_total = reduce_first(strips)
    own_tile, near_tile = reduce_second([own_total, near_total])
    strips = tile_products(
        far + other_far, weighted + other_weighted, halved, split=True, windowed=True
    )
    (far_tile,) = reduce_second([reduce_first(strips)])

    own_tile, near_tile = lax.optimization_barrier((own_tile, near_tile))

    def fetch(value, place):
        return lax.ppermute(value, AXES, homes(place))

    own = [fetch(own_tile, own_source(part)) for part in (0, 1)]
    direct = [fetch(near_tile, near_source(half, False)) for half in (0, 1)]
    padded = jnp.concatenate([far_tile, far_tile], axis=0)
    odd = xl ^ xh ^ core
    chosen = [jnp.where(odd == half, near_tile, padded) for half in (0, 1)]
    mixed = [
        fetch(chosen[half], both(near_source(half, True), far_source(half, 1)))
        for half in (0, 1)
    ]
    two = [fetch(far_tile, far_source(half, 0)) for half in (0, 1)]
    return finish(whole, *direct, *mixed, *two, *own)


def solution(mesh):
    fine = Mesh(mesh.devices.reshape(SIZES), AXES)

    return jax.shard_map(
        body,
        mesh=fine,
        in_specs=(P(AXES, None), P(AXES), P(AXES), P(), P(), P(), P()),
        out_specs=P(("xh", "y", "core"), ("xl", "z")),
        check_vma=False,
    )
```
